32 devices in a mesh: rep: 8 (over y, x, core), shard: 4 (over z).
Axes of the slice: x: 2, y: 2, z: 4, core: 2. Of those that a mesh axis runs over, the one named last changes fastest.
Arguments:
- tokens: bfloat16 [4096, 768], P(('rep', 'shard')), may hold values from -30 to 30
- segments: int32 [32, 128], P(('rep', 'shard')), may hold values from 0 to 7, never falling along the last dimension, each value on 1 to 64 neighbouring positions
- w_query: bfloat16 [768, 768], P('shard'), may hold values from -0.21875 to 0.21875
- w_key: bfloat16 [768, 768], P('shard'), may hold values from -0.21875 to 0.21875
- w_value: bfloat16 [768, 768], P('shard'), may hold values from -0.21875 to 0.21875
- w_out: bfloat16 [768, 768], P('shard'), may hold values from -0.875 to 0.875
- b_query: bfloat16 [768], P('shard'), may hold values from -3 to 3
- b_value: bfloat16 [768], P('shard'), may hold values from -3 to 3
- b_out: bfloat16 [768], P('shard'), may hold values from -3 to 3
- gain_one: bfloat16 [768], P('shard'), may hold values from 0.099609375 to 1.8984375
- shift_one: bfloat16 [768], P('shard'), may hold values from -3 to 3
- w_up: bfloat16 [768, 3072], P('shard'), may hold values from -0.21875 to 0.21875
- b_up: bfloat16 [3072], P('shard'), may hold values from -3 to 3
- w_down: bfloat16 [3072, 768], P('shard'), may hold values from -0.109375 to 0.109375
- b_down: bfloat16 [768], P('shard'), may hold values from -3 to 3
- gain_two: bfloat16 [768], P('shard'), may hold values from 0.099609375 to 1.8984375
- shift_two: bfloat16 [768], P('shard'), may hold values from -3 to 3
- cotangent: bfloat16 [4096, 768], P(('rep', 'shard')), may hold values from -6 to 6
Outputs:
- output: bfloat16 [4096, 768], P(('rep', 'shard'))
- grad_tokens: bfloat16 [4096, 768], P(('rep', 'shard'))
- grad_w_query: float32 [768, 768], P('shard')
- grad_w_key: float32 [768, 768], P('shard')
- grad_w_value: float32 [768, 768], P('shard')
- grad_w_out: float32 [768, 768], P('shard')
- grad_b_query: float32 [768], P('shard')
- grad_b_value: float32 [768], P('shard')
- grad_b_out: float32 [768], P('shard')
- grad_gain_one: float32 [768], P('shard')
- grad_shift_one: float32 [768], P('shard')
- grad_w_up: float32 [768, 3072], P('shard')
- grad_b_up: float32 [3072], P('shard')
- grad_w_down: float32 [3072, 768], P('shard')
- grad_b_down: float32 [768], P('shard')
- grad_gain_two: float32 [768], P('shard')
- grad_shift_two: float32 [768], P('shard')
The draws below stay inside these ranges and needn't reach their ends.
Inputs may be any that keep to these rules, and one draw needn't show every extreme that they name: `segments`: segment numbers never fall along a row; each segment holds 1 to 64 tokens, and in every row exactly one segment holds 64 tokens.
All inputs are finite; a program needn't handle non-finite values.
Results may differ from the reference program's by a relative error of at most 0.014.
The reference program's roundings to bfloat16 on the way (of `probs`, `context`, `norm_one_b`, `act`, `g_context` and `g_scores`) count: a program that leaves them out, or rounds other values in their place, can miss the bound.
Values may be sent and summed in bfloat16 or wider, within the bound.
A program may use at most 128 MiB of HBM per device.

```python
import math
import jax
import jax.numpy as jnp
import numpy as np
from jax import lax

D = 768
HEAD_DIM = 64
FF = 3072
SEQ = 128
ROWS = 32
TOKENS = 4096


def draw_tokens(key, part):
    base = jnp.clip(jax.random.normal(key, (TOKENS, D), jnp.float32), -5.0, 5.0)
    return base.astype(jnp.bfloat16)


def block_scale(own_key, shape, split, smallest, largest):
    def one(axis_at, parts):
        steps = jax.random.uniform(jax.random.fold_in(jax.random.fold_in(own_key, 6), axis_at), (parts,), jnp.float32, smallest / len(split), largest / len(split))
        return jnp.repeat(jnp.exp(steps), shape[axis_at] // parts).reshape((-1,) + (1,) * (len(shape) - axis_at - 1))

    factor_of = one(*split[0])
    for cut in split[1:]:
        factor_of = factor_of * one(*cut)
    return factor_of


def split_up(amount, total, reach, skew):
    loads = [(1 << 20) // math.isqrt(rank ** skew) + 1 for rank in range(2, amount + 1)]
    rest, holding = total - reach - (amount - 1), [1] * (amount - 1)
    while rest > 0:
        movable = [i for i in range(amount - 1) if holding[i] < reach]
        pool, budget = sum([loads[i] for i in movable]), rest
        for i in movable:
            extra = min(reach - holding[i], max(1, budget * loads[i] // pool), rest)
            holding[i] = holding[i] + extra
            rest = rest - extra
    return np.array([reach] + holding)


def uneven_parts(stream_key, number_of, total, reach, skew):
    if number_of == 2:
        one = jax.random.randint(stream_key, (), max(1, total - reach), min(reach, total - 1) + 1)
        return jnp.stack([one, total - one])
    lengths = jnp.asarray(split_up(number_of, total, reach, skew), jnp.int32)
    pairs = (number_of - 1) // 2
    donor, taker = lengths[1:1 + 2 * pairs:2], lengths[2:2 + 2 * pairs:2]
    slack = jnp.minimum(donor - 1, reach - taker)
    moved = jax.random.randint(jax.random.fold_in(stream_key, 1), (pairs,), 0, 1 << 20) % (slack + 1)
    lengths = lengths.at[1:1 + 2 * pairs:2].set(donor - moved).at[2:2 + 2 * pairs:2].set(taker + moved)
    return lengths[jax.random.permutation(jax.random.fold_in(stream_key, 2), number_of)]


def scatter_about(rng, extent, spread, most, pieces=(), dtype=jnp.bfloat16):
    entries = spread * jax.random.normal(rng, extent, jnp.float32)
    if pieces:
        entries = entries * block_scale(rng, extent, pieces, -0.22, 0.18)
    return jnp.clip(entries, -most, most).astype(dtype)


def setup_inputs(seed: int = 0) -> dict:
    key_of = jax.random.split(jax.random.key(seed), 19)
    return {
        "tokens": draw_tokens(jax.random.fold_in(key_of[18], 71), 0),
        "segments": jax.vmap(lambda own: jnp.searchsorted(jnp.cumsum(uneven_parts(own, 8, SEQ, SEQ // 2, 0)), jnp.arange(SEQ), side="right"))(jax.random.split(key_of[1], ROWS)).reshape((ROWS, SEQ)).astype(jnp.int32),
        "w_query": scatter_about(key_of[2], (D, D), D ** -0.5, 0.21875, ((0, 4),)),
        "w_key": scatter_about(key_of[3], (D, D), D ** -0.5, 0.21875, ((0, 4),)),
        "w_value": scatter_about(key_of[4], (D, D), D ** -0.5, 0.21875, ((0, 4),)),
        "w_out": scatter_about(key_of[5], (D, D), (D // 16) ** -0.5, 0.875, ((0, 4),)),
        "b_query": scatter_about(key_of[6], (D,), 0.5, 3.0, ((0, 4),)),
        "b_value": scatter_about(key_of[7], (D,), 0.5, 3.0, ((0, 4),)),
        "b_out": scatter_about(key_of[8], (D,), 0.5, 3.0, ((0, 4),)),
        "gain_one": jnp.clip(1.0 + 0.18 * jax.random.normal(key_of[9], (D,), jnp.float32), 0.099609375, 1.8984375).astype(jnp.bfloat16),
        "shift_one": scatter_about(key_of[10], (D,), 0.5, 3.0, ((0, 4),)),
        "w_up": scatter_about(key_of[11], (D, FF), D ** -0.5, 0.21875, ((0, 4),)),
        "b_up": scatter_about(key_of[12], (FF,), 0.5, 3.0, ((0, 4),)),
        "w_down": scatter_about(key_of[13], (FF, D), FF ** -0.5, 0.109375, ((0, 4),)),
        "b_down": scatter_about(key_of[14], (D,), 0.5, 3.0, ((0, 4),)),
        "gain_two": jnp.clip(1.0 + 0.18 * jax.random.normal(key_of[15], (D,), jnp.float32), 0.099609375, 1.8984375).astype(jnp.bfloat16),
        "shift_two": scatter_about(key_of[16], (D,), 0.5, 3.0, ((0, 4),)),
        "cotangent": scatter_about(key_of[17], (TOKENS, D), 1.0, 6.0, ((0, 32),)),
    }


epsilon = 1e-05
masked_value = -1e+30
root_half = 0.7071067811865476
inv_root_tau = 0.3989422804014327

def layer_norm(hidden, gain, shift):
    center = hidden - lax.optimization_barrier(jnp.mean(hidden, axis=-1, keepdims=True))
    inv_std = lax.rsqrt(lax.optimization_barrier(jnp.mean(center * center, axis=-1, keepdims=True)) + epsilon)
    normed = center * inv_std
    return (normed * gain + shift, normed, inv_std)

def norm_back(upstream, normed, inv_std, gain):
    scaled = upstream * gain
    grad_in = inv_std * (scaled - lax.optimization_barrier(jnp.mean(scaled, axis=-1, keepdims=True)) - normed * lax.optimization_barrier(jnp.mean(scaled * normed, axis=-1, keepdims=True)))
    return (grad_in, lax.optimization_barrier(jnp.sum(upstream * normed, axis=0)), lax.optimization_barrier(jnp.sum(upstream, axis=0)))

def gelu_value(pre):
    return 0.5 * pre * (1.0 + lax.erf(pre * root_half))

def gelu_slope(pre):
    return 0.5 * (1.0 + lax.erf(pre * root_half)) + pre * jnp.exp(-0.5 * pre * pre) * inv_root_tau

def masked_scores(queries, keys, seg_block, scale):
    scores = jnp.einsum('gqhe,gkhe->ghqk', queries.astype(jnp.float32), keys.astype(jnp.float32)) * scale
    allowed = (seg_block[:, :, None] == seg_block[:, None, :])[:, None]
    return jnp.where(allowed, scores, masked_value)

def dense(left, right):
    return jnp.dot(left, right, preferred_element_type=jnp.float32)

def reference(tokens, segments, w_query, w_key, w_value, w_out, b_query, b_value, b_out, gain_one, shift_one, w_up, b_up, w_down, b_down, gain_two, shift_two, cotangent):
    group = math.gcd(ROWS, max(1, 4096 // SEQ))
    blocks = ROWS // group
    heads_count = D // HEAD_DIM
    scale = 1.0 / math.sqrt(HEAD_DIM)
    f32 = jnp.float32
    bf16 = jnp.bfloat16

    def split_heads(matrix):
        return matrix.reshape(group, SEQ, heads_count, HEAD_DIM)

    def one_group(totals, inputs):
        block, seg_block, grad_block = inputs
        queries = (dense(block, w_query) + b_query.astype(f32)).astype(bf16)
        keys = dense(block, w_key).astype(bf16)
        values = (dense(block, w_value) + b_value.astype(f32)).astype(bf16)
        q_heads, k_heads, v_heads = (split_heads(queries), split_heads(keys), split_heads(values))
        scores = masked_scores(q_heads, k_heads, seg_block, scale)
        top = lax.optimization_barrier(jnp.max(scores, axis=-1, keepdims=True))
        log_total = top + jnp.log(lax.optimization_barrier(jnp.sum(jnp.exp(scores - top), axis=-1, keepdims=True)))
        probs = jnp.exp(scores - log_total).astype(bf16)
        context = jnp.einsum('ghqk,gkhe->gqhe', probs.astype(f32), v_heads.astype(f32)).astype(bf16).reshape(-1, D)
        resid_one = block.astype(f32) + dense(context, w_out) + b_out.astype(f32)
        norm_one, normed_one, inv_one = layer_norm(resid_one, gain_one.astype(f32), shift_one.astype(f32))
        norm_one_b = norm_one.astype(bf16)
        pre_act = dense(norm_one_b, w_up) + b_up.astype(f32)
        act = gelu_value(pre_act).astype(bf16)
        resid_two = norm_one + dense(act, w_down) + b_down.astype(f32)
        final, normed_two, inv_two = layer_norm(resid_two, gain_two.astype(f32), shift_two.astype(f32))
        output = final.astype(bf16)
        g_resid_two, g_gain_two, g_shift_two = norm_back(grad_block.astype(f32), normed_two, inv_two, gain_two.astype(f32))
        g_two_b = g_resid_two.astype(bf16)
        g_w_down = dense(act.T, g_two_b)
        g_b_down = lax.optimization_barrier(jnp.sum(g_resid_two, axis=0))
        g_pre = dense(g_two_b, w_down.T) * gelu_slope(pre_act)
        g_b_up = lax.optimization_barrier(jnp.sum(g_pre, axis=0))
        g_pre_b = g_pre.astype(bf16)
        g_w_up = dense(norm_one_b.T, g_pre_b)
        g_norm_one = g_resid_two + dense(g_pre_b, w_up.T)
        g_resid_one, g_gain_one, g_shift_one = norm_back(g_norm_one, normed_one, inv_one, gain_one.astype(f32))
        g_one_b = g_resid_one.astype(bf16)
        g_w_out = dense(context.T, g_one_b)
        g_b_out = lax.optimization_barrier(jnp.sum(g_resid_one, axis=0))
        g_context = split_heads(dense(g_one_b, w_out.T).astype(bf16))
        probs_f = jnp.exp(masked_scores(q_heads, k_heads, seg_block, scale) - log_total)
        probs_b = probs_f.astype(bf16)
        g_probs = jnp.einsum('gqhe,gkhe->ghqk', g_context.astype(f32), v_heads.astype(f32))
        delta = lax.optimization_barrier(jnp.sum(probs_f * g_probs, axis=-1, keepdims=True))
        g_scores = (probs_f * (g_probs - delta) * scale).astype(bf16)
        g_queries = jnp.einsum('ghqk,gkhe->gqhe', g_scores.astype(f32), k_heads.astype(f32)).reshape(-1, D)
        g_keys = jnp.einsum('ghqk,gqhe->gkhe', g_scores.astype(f32), q_heads.astype(f32)).reshape(-1, D)
        g_values = jnp.einsum('ghqk,gqhe->gkhe', probs_b.astype(f32), g_context.astype(f32)).reshape(-1, D)
        g_b_query = lax.optimization_barrier(jnp.sum(g_queries, axis=0))
        g_b_value = lax.optimization_barrier(jnp.sum(g_values, axis=0))
        gq_b, gk_b, gv_b = (g_queries.astype(bf16), g_keys.astype(bf16), g_values.astype(bf16))
        g_w_query = dense(block.T, gq_b)
        g_w_key = dense(block.T, gk_b)
        g_w_value = dense(block.T, gv_b)
        g_input = (g_resid_one + dense(gq_b, w_query.T) + dense(gk_b, w_key.T) + dense(gv_b, w_value.T)).astype(bf16)
        terms = (g_w_query, g_w_key, g_w_value, g_w_out, g_b_query, g_b_value, g_b_out, g_gain_one, g_shift_one, g_w_up, g_b_up, g_w_down, g_b_down, g_gain_two, g_shift_two)
        new_totals = tuple((total + term for total, term in zip(totals, terms)))
        return (new_totals, (output, g_input))
    shapes = [(D, D), (D, D), (D, D), (D, D), (D,), (D,), (D,), (D,), (D,), (D, FF), (FF,), (FF, D), (D,), (D,), (D,)]
    start = tuple((jnp.zeros(shape, jnp.float32) for shape in shapes))
    inputs = (tokens.reshape(blocks, group * SEQ, D), segments.reshape(blocks, group, SEQ), cotangent.reshape(blocks, group * SEQ, D))
    totals, (outputs, grads) = lax.scan(one_group, start, inputs)
    return (outputs.reshape(TOKENS, D), grads.reshape(TOKENS, D), totals[0], totals[1], totals[2], totals[3], totals[4], totals[5], totals[6], totals[7], totals[8], totals[9], totals[10], totals[11], totals[12], totals[13], totals[14])
```

```python
import functools
import math

import jax
import jax.numpy as jnp
from jax import lax
from jax.sharding import PartitionSpec as P

HEAD_DIM = 64


epsilon = 1e-05
masked_value = -1e30
root_half = 0.7071067811865476
inv_root_tau = 0.3989422804014327


def layer_norm(hidden, gain, shift):
    center = hidden - jnp.mean(hidden, axis=-1, keepdims=True)
    inv_std = lax.rsqrt(jnp.mean(center * center, axis=-1, keepdims=True) + epsilon)
    normed = center * inv_std
    return (normed * gain + shift, normed, inv_std)


def norm_back(upstream, normed, inv_std, gain):
    scaled = upstream * gain
    grad_in = inv_std * (
        scaled
        - jnp.mean(scaled, axis=-1, keepdims=True)
        - normed * jnp.mean(scaled * normed, axis=-1, keepdims=True)
    )
    return (grad_in, jnp.sum(upstream * normed, axis=0), jnp.sum(upstream, axis=0))


def gelu_value(pre):
    return 0.5 * pre * (1.0 + lax.erf(pre * root_half))


def gelu_slope(pre):
    return 0.5 * (1.0 + lax.erf(pre * root_half)) + pre * jnp.exp(-0.5 * pre * pre) * inv_root_tau


def masked_scores(queries, keys, seg_block, scale):
    scores = (
        jnp.einsum("gqhe,gkhe->ghqk", queries, keys, preferred_element_type=jnp.float32) * scale
    )
    allowed = (seg_block[:, :, None] == seg_block[:, None, :])[:, None]
    return jnp.where(allowed, scores, masked_value)


def dense(left, right):
    return jnp.dot(left, right, preferred_element_type=jnp.float32)


def bit_of(value, bit):
    return (value // bit) % 2


class Net:
    def __init__(self, reps, shards):
        self.reps, self.shards = reps, shards
        self.rep = lax.axis_index("rep")
        self.shard = lax.axis_index("shard")
        self.core = self.rep % 2
        bits = []
        bit = 2
        while bit < reps:
            bits.append(bit)
            bit = bit * 2
        self.orders = (tuple(bits), tuple(reversed(bits)))
        self.steps = len(bits)

    def permute(self, array, partner):
        pairs = []
        for r in range(self.reps):
            for s in range(self.shards):
                pr, ps = partner(r, s)
                pairs.append((r * self.shards + s, pr * self.shards + ps))
        return lax.ppermute(array, ("rep", "shard"), pairs)

    def flip_core(self, array):
        return self.permute(array, lambda r, s: (r ^ 1, s))

    def flip_step(self, array, i):
        return self.permute(array, lambda r, s: (r ^ self.orders[r % 2][i], s))

    def flip_shard(self, array, k):
        return self.permute(array, lambda r, s: (r, s ^ k))

    def flip_bit(self, array, bit):
        return self.permute(array, lambda r, s: (r ^ bit, s))

    def my_bit(self, i):
        return jnp.where(
            self.core == 0,
            bit_of(self.rep, self.orders[0][i]),
            bit_of(self.rep, self.orders[1][i]),
        )

    def my_part(self):
        part = 0
        for i in range(self.steps):
            part = part * 2 + self.my_bit(i)
        return part


def ordered(bit, mine, theirs, axis):
    return jnp.where(
        bit == 0,
        jnp.concatenate([mine, theirs], axis),
        jnp.concatenate([theirs, mine], axis),
    )


def after(array, *others):
    return lax.optimization_barrier((array, *others))[0]


def weight_piece(net, own):
    rows, columns = own.shape
    here, half = rows // (net.reps // 2), columns // 2
    return lax.dynamic_slice(own, (net.my_part() * here, net.core * half), (here, half))


def over_shards(net, piece):
    return [net.flip_shard(piece, k) for k in range(1, net.shards)]


def gather_weight(net, own, arrived):
    rows, columns = own.shape
    half = columns // 2
    arrived = jnp.stack(arrived)
    for i in reversed(range(net.steps)):
        arrived = ordered(net.my_bit(i), arrived, net.flip_step(arrived, i), 1)
    other = net.flip_core(arrived)
    full = jnp.zeros((net.shards * rows, columns), own.dtype)
    full = lax.dynamic_update_slice(full, own, (net.shard * rows, 0))
    for k in range(1, net.shards):
        at = (net.shard ^ k) * rows
        full = lax.dynamic_update_slice(full, arrived[k - 1], (at, net.core * half))
        full = lax.dynamic_update_slice(full, other[k - 1], (at, (1 - net.core) * half))
    return full


def in_shard_order(net, own, arrived):
    full = jnp.zeros((net.shards, own.shape[0]), own.dtype)
    full = lax.dynamic_update_slice(full, own[None], (net.shard, 0))
    for k in range(1, net.shards):
        full = lax.dynamic_update_slice(full, arrived[k - 1][None], (net.shard ^ k, 0))
    return full


def halve(net, now, i):
    parts = now.shape[1] // 2
    mine = lax.dynamic_slice_in_dim(now, net.my_bit(i) * parts, parts, 1)
    sent = lax.dynamic_slice_in_dim(now, (1 - net.my_bit(i)) * parts, parts, 1)
    return mine, sent


def halved(net, mine, sent, i):
    f32 = jnp.float32
    return (mine.astype(f32) + net.flip_step(sent, i).astype(f32)).astype(jnp.bfloat16)


def split_rows(net, total):
    rows, half = total.shape
    parts = net.reps // 2
    return total.reshape(net.shards, parts, rows // net.shards // parts, half)


def reduce_rest(net, now, first):
    f32 = jnp.float32
    bf16 = jnp.bfloat16
    for i in range(first, net.steps):
        now = halved(net, *halve(net, now, i), i)
    now = now.reshape(net.shards, now.shape[2], now.shape[3])
    kept = lax.dynamic_index_in_dim(now, net.shard, 0, keepdims=False).astype(f32)
    for k in range(1, net.shards):
        sent = lax.dynamic_index_in_dim(now, net.shard ^ k, 0, keepdims=False)
        kept = kept + net.flip_shard(sent, k).astype(f32)
    done = lax.optimization_barrier(kept.astype(bf16))
    for i in reversed(range(net.steps)):
        done = ordered(net.my_bit(i), done, net.flip_step(done, i), 0)
    other = net.flip_core(done)
    return ordered(net.core, done, other, 1).astype(f32)


def sum_vectors(net, vector):
    for k in (1, 2):
        if k < net.shards:
            vector = vector + net.flip_shard(vector, k)
    bit = 1
    while bit < net.reps:
        vector = vector + net.flip_bit(vector, bit)
        bit = bit * 2
    return vector


def paired(net, mine, sent):
    return jnp.concatenate([mine, net.flip_core(sent)], 0)


def body(
    reps,
    shards,
    tokens,
    segments,
    w_query,
    w_key,
    w_value,
    w_out,
    b_query,
    b_value,
    b_out,
    gain_one,
    shift_one,
    w_up,
    b_up,
    w_down,
    b_down,
    gain_two,
    shift_two,
    cotangent,
):
    f32 = jnp.float32
    bf16 = jnp.bfloat16
    net = Net(reps, shards)
    width = tokens.shape[1]
    own_rows = w_query.shape[0]
    vec_own = jnp.concatenate(
        [b_query, b_value, b_out, gain_one, shift_one, b_down, gain_two, shift_two, b_up]
    )
    own_attn = jnp.concatenate([w_query, w_key, w_value, w_out], 1)
    piece = weight_piece(net, own_attn)
    rows_piece, half = piece.shape
    extra = -(-vec_own.shape[0] // half)
    riding = jnp.pad(vec_own, (0, extra * half - vec_own.shape[0])).reshape(extra, half)
    over_attn = over_shards(net, jnp.concatenate([piece, riding], 0))
    over_up = over_shards(net, after(weight_piece(net, w_up), *over_attn))
    over_down = over_shards(net, after(weight_piece(net, w_down), *over_up))
    vec_all = in_shard_order(
        net,
        vec_own,
        [one[rows_piece:].reshape(-1)[: vec_own.shape[0]] for one in over_attn],
    )

    def vector_at(i):
        return vec_all[:, i * own_rows : (i + 1) * own_rows].reshape(-1)

    bias_query, bias_value, bias_out, full_gain_one = (vector_at(i) for i in range(4))
    full_shift_one, bias_down, full_gain_two, full_shift_two = (vector_at(i) for i in range(4, 8))
    bias_up = vec_all[:, 8 * own_rows :].reshape(-1)
    full_attn = gather_weight(net, own_attn, [one[:rows_piece] for one in over_attn])
    full_up = gather_weight(net, w_up, over_up)
    full_down = gather_weight(net, w_down, over_down)
    core = net.core

    def half_of(matrix, which):
        size = matrix.shape[1] // 2
        return lax.dynamic_slice_in_dim(matrix, which * size, size, 1)

    full_query, full_key, full_value, full_out = (
        full_attn[:, i * width : (i + 1) * width] for i in range(4)
    )
    rows_here, seq_len = segments.shape
    heads_count = width // HEAD_DIM
    scale = 1.0 / math.sqrt(HEAD_DIM)

    def split_heads(matrix):
        return matrix.reshape(rows_here, seq_len, heads_count, HEAD_DIM)

    queries = (dense(tokens, full_query) + bias_query.astype(f32)).astype(bf16)
    keys = dense(tokens, full_key).astype(bf16)
    values = (dense(tokens, full_value) + bias_value.astype(f32)).astype(bf16)
    q_heads, k_heads, v_heads = (split_heads(queries), split_heads(keys), split_heads(values))
    scores = masked_scores(q_heads, k_heads, segments, scale)
    top = jnp.max(scores, axis=-1, keepdims=True)
    log_total = top + jnp.log(jnp.sum(jnp.exp(scores - top), axis=-1, keepdims=True))
    probs = jnp.exp(scores - log_total).astype(bf16)
    context = (
        jnp.einsum("ghqk,gkhe->gqhe", probs, v_heads, preferred_element_type=f32)
        .astype(bf16)
        .reshape(-1, width)
    )
    resid_one = tokens.astype(f32) + dense(context, full_out) + bias_out.astype(f32)
    norm_one, normed_one, inv_one = layer_norm(
        resid_one, full_gain_one.astype(f32), full_shift_one.astype(f32)
    )
    norm_one_b = norm_one.astype(bf16)
    pre_act = dense(norm_one_b, full_up) + bias_up.astype(f32)
    act = gelu_value(pre_act).astype(bf16)
    resid_two = norm_one + dense(act, full_down) + bias_down.astype(f32)
    final, normed_two, inv_two = layer_norm(
        resid_two, full_gain_two.astype(f32), full_shift_two.astype(f32)
    )
    output = final.astype(bf16)
    back_query, back_key, back_value, back_out = (full_query, full_key, full_value, full_out)
    back_up, back_down, back_gain_one, back_gain_two = (
        full_up,
        full_down,
        full_gain_one,
        full_gain_two,
    )
    g_resid_two, g_gain_two, g_shift_two = norm_back(
        cotangent.astype(f32), normed_two, inv_two, back_gain_two.astype(f32)
    )
    g_two_b = g_resid_two.astype(bf16)
    g_b_down = jnp.sum(g_resid_two, axis=0)
    pair_act = paired(net, act, act)
    pair_two = paired(net, half_of(g_two_b, core), half_of(g_two_b, 1 - core))
    down_now = split_rows(net, dense(pair_act.T, pair_two).astype(bf16))
    down_mine, down_sent = halve(net, down_now, 0)
    g_pre = dense(g_two_b, back_down.T) * gelu_slope(pre_act)
    g_b_up = jnp.sum(g_pre, axis=0)
    g_pre_b = g_pre.astype(bf16)
    pair_norm = paired(net, norm_one_b, norm_one_b)
    pair_pre = paired(net, half_of(g_pre_b, core), half_of(g_pre_b, 1 - core))
    down_now = halved(net, down_mine, down_sent, 0)
    g_norm_one = g_resid_two + dense(after(g_pre_b, down_sent), back_up.T)
    g_resid_one, g_gain_one, g_shift_one = norm_back(
        g_norm_one, normed_one, inv_one, back_gain_one.astype(f32)
    )
    g_one_b = g_resid_one.astype(bf16)
    g_b_out = jnp.sum(g_resid_one, axis=0)
    up_now = split_rows(net, dense(pair_norm.T, pair_pre).astype(bf16))
    up_mine, up_sent = halve(net, up_now, 0)
    up_sent = after(up_sent, down_now)
    up_now = halved(net, up_mine, up_sent, 0)
    g_one_b = after(g_one_b, up_sent)
    g_context = split_heads(dense(g_one_b, back_out.T).astype(bf16))
    probs_f = jnp.exp(masked_scores(q_heads, k_heads, segments, scale) - log_total)
    probs_b = probs_f.astype(bf16)
    g_probs = jnp.einsum("gqhe,gkhe->ghqk", g_context, v_heads, preferred_element_type=f32)
    delta = jnp.sum(probs_f * g_probs, axis=-1, keepdims=True)
    g_scores = (probs_f * (g_probs - delta) * scale).astype(bf16)
    g_queries = jnp.einsum(
        "ghqk,gkhe->gqhe", g_scores, k_heads, preferred_element_type=f32
    ).reshape(-1, width)
    g_keys = jnp.einsum("ghqk,gqhe->gkhe", g_scores, q_heads, preferred_element_type=f32).reshape(
        -1, width
    )
    g_values = jnp.einsum(
        "ghqk,gqhe->gkhe", probs_b, g_context, preferred_element_type=f32
    ).reshape(-1, width)
    g_b_query = jnp.sum(g_queries, axis=0)
    g_b_value = jnp.sum(g_values, axis=0)
    gq_b, gk_b, gv_b = (g_queries.astype(bf16), g_keys.astype(bf16), g_values.astype(bf16))
    grad_tokens = (
        g_resid_one
        + dense(gq_b, back_query.T)
        + dense(gk_b, back_key.T)
        + dense(gv_b, back_value.T)
    ).astype(bf16)
    pair_tokens = paired(net, tokens, tokens)
    pair_context = paired(net, context, context)
    at_first = core == 0
    gq_b = after(gq_b, up_now)
    pair_right_one = paired(
        net, jnp.where(at_first, gq_b, gv_b), jnp.where(at_first, gv_b, gq_b)
    )
    pair_right_two = paired(
        net, jnp.where(at_first, gk_b, g_one_b), jnp.where(at_first, g_one_b, gk_b)
    )
    pair_left_two = jnp.where(at_first, pair_tokens, pair_context)
    attn_now = split_rows(
        net,
        jnp.concatenate(
            [
                dense(pair_tokens.T, pair_right_one).astype(bf16),
                dense(pair_left_two.T, pair_right_two).astype(bf16),
            ],
            1,
        ),
    )
    own_down = reduce_rest(net, down_now, 1)
    own_up = reduce_rest(net, up_now, 1)
    own_attn = reduce_rest(net, attn_now, 0)
    vec_grads = (
        g_b_query,
        g_b_value,
        g_b_out,
        g_gain_one,
        g_shift_one,
        g_b_up,
        g_b_down,
        g_gain_two,
        g_shift_two,
    )
    summed = sum_vectors(net, after(jnp.concatenate(vec_grads), attn_now))
    own_vecs = []
    at = 0
    for one in vec_grads:
        size = one.shape[0] // shards
        own_vecs.append(lax.dynamic_slice_in_dim(summed, at + net.shard * size, size))
        at = at + one.shape[0]
    return (
        output,
        grad_tokens,
        own_attn[:, :width],
        own_attn[:, width : 2 * width],
        own_attn[:, 2 * width : 3 * width],
        own_attn[:, 3 * width :],
        own_vecs[0],
        own_vecs[1],
        own_vecs[2],
        own_vecs[3],
        own_vecs[4],
        own_up,
        own_vecs[5],
        own_down,
        own_vecs[6],
        own_vecs[7],
        own_vecs[8],
    )


def solution(mesh):
    return jax.shard_map(
        functools.partial(body, mesh.shape["rep"], mesh.shape["shard"]),
        mesh=mesh,
        in_specs=(
            P(("rep", "shard"), None),
            P(("rep", "shard"), None),
            P("shard", None),
            P("shard", None),
            P("shard", None),
            P("shard", None),
            P("shard"),
            P("shard"),
            P("shard"),
            P("shard"),
            P("shard"),
            P("shard", None),
            P("shard"),
            P("shard", None),
            P("shard"),
            P("shard"),
            P("shard"),
            P(("rep", "shard"), None),
        ),
        out_specs=(
            P(("rep", "shard"), None),
            P(("rep", "shard"), None),
            P("shard", None),
            P("shard", None),
            P("shard", None),
            P("shard", None),
            P("shard"),
            P("shard"),
            P("shard"),
            P("shard"),
            P("shard"),
            P("shard", None),
            P("shard"),
            P("shard", None),
            P("shard"),
            P("shard"),
            P("shard"),
        ),
        check_vma=False,
    )
```
